512 devices in a mesh: row: 32 (over y, z_lo), col: 16 (over x, z_hi, core).
Axes of the slice: x: 4, y: 8, z: 8 (z_hi: 2, z_lo: 4; z = z_hi * 4 + z_lo), core: 2. Of those that a mesh axis runs over, the one named last changes fastest.
Arguments:
- covariance: float32 [8192, 8192], P('row', 'col')
- courants: float32 [2, 2, 64, 128], replicated, may hold values from -0.9 to 0.9
- process_noise_spread: float32 [64, 128], P('row'), may hold values from 0.1 to 1
- sensor_targets: int32 [512], replicated, may hold values from 0 to 8191, as said below
- noise_variance: float32 [512], replicated, may hold values from 0.2 to 1
Outputs:
- posterior_spread: float32 [8192, 8192], P('row', 'col')
The draws below stay inside these ranges and needn't reach their ends.
Inputs may be any that keep to these rules, and one draw needn't show every extreme that they name: `sensor_targets`: sorted ascending, all distinct; exactly 16 of them lie in each band of 256 consecutive state indices that starts at a multiple of 256.
All inputs are finite; a program needn't handle non-finite values.
Results may differ from the reference program's by a relative error of at most 0.0003.
Values sent between devices are 32-bit elements; how exact they have to be, the bound alone decides.
No kernel may reach another device: no remote copies, remote signals or barrier semaphores. Data moves between devices by JAX's collectives and lax.ppermute only.
A program may use at most 64 MiB of HBM per device.

```python
import math
import jax
import jax.numpy as jnp
from jax import lax

NC = 128
ROWS_DEV = 2
OBS_DEV = 16
CYCLES = 2
NR = 64
OBS = 512


def draw_covariance(key, part):
    system_snapshots = NR * NC
    gaussian = jax.random.normal(jax.random.fold_in(key, 11), (system_snapshots, system_snapshots), jnp.float32)
    rough_part = (gaussian + gaussian.T) * (0.4 / math.sqrt(2.0 * system_snapshots))
    variance = jax.random.uniform(jax.random.fold_in(key, 12), (system_snapshots,), jnp.float32, 1.2, 2.4)
    positions = jnp.arange(system_snapshots, dtype=jnp.int32)
    result = rough_part.at[positions, positions].set(variance)
    return result


def draw_sensor_targets(key, part):
    band_cells = ROWS_DEV * NC
    band_total = OBS // OBS_DEV
    band_keys = jax.random.split(jax.random.fold_in(key, 21), band_total)

    def choose(subkey):
        return jnp.sort(jax.random.permutation(subkey, band_cells)[:OBS_DEV].astype(jnp.int32))
    chosen = jax.vmap(choose)(band_keys)
    offsets = jnp.arange(band_total, dtype=jnp.int32)[:, None] * band_cells
    return (chosen + offsets).reshape(OBS).astype(jnp.int32)


def shard_levels(rng, extent, shards, smallest, largest):
    gain, own = 1.0, jax.random.fold_in(rng, 6)
    for axis_at, shards_of in shards:
        heights = jnp.exp(jax.random.uniform(jax.random.fold_in(own, axis_at), (shards_of,), jnp.float32, smallest / len(shards), largest / len(shards)))
        gain = gain * jnp.repeat(heights, extent[axis_at] // shards_of).reshape([-1 if axis == axis_at else 1 for axis in range(len(extent))])
    return gain


def setup_inputs(seed: int = 0) -> dict:
    arg_keys = jax.random.split(jax.random.key(seed), 6)
    return {
        "covariance": draw_covariance(jax.random.fold_in(arg_keys[5], 71), 0),
        "courants": jnp.clip(jax.random.uniform(arg_keys[1], (CYCLES, 2, NR, NC), jnp.float32, -0.9, 0.9), -0.9, 0.9),
        "process_noise_spread": jnp.clip(jnp.exp(math.log(1.0) - 2.3025851 * jax.random.uniform(arg_keys[2], (NR, NC), jnp.float32) ** shard_levels(arg_keys[2], (NR, NC), ((0, 32),), -0.2, 0.2)), 0.1, 1.0),
        "sensor_targets": draw_sensor_targets(jax.random.fold_in(arg_keys[5], 71), 0),
        "noise_variance": jnp.clip(jnp.exp(jax.random.uniform(arg_keys[4], (OBS,), jnp.float32, math.log(0.2), math.log(1.0))), 0.2, 1.0),
    }


finest_accuracy = lax.Precision.HIGHEST

def stencil_weights(courant):
    return (courant * (1.0 + courant) * 0.5, 1.0 - courant * courant, courant * (courant - 1.0) * 0.5)

def sweep_local(joint_spread_array, courant, which_axis):
    weight_behind, weight_centre, weight_ahead = stencil_weights(courant)
    return weight_behind * jnp.roll(joint_spread_array, 1, which_axis) + weight_centre * joint_spread_array + weight_ahead * jnp.roll(joint_spread_array, -1, which_axis)

def reference(covariance, courants, process_noise_spread, sensor_targets, noise_variance):
    system_snapshots = NR * NC
    wrapped_mesh = covariance.reshape(NR, NC, NR, NC)
    for cycle_index in range(CYCLES):
        eastward = courants[cycle_index, 0]
        northward = courants[cycle_index, 1]
        wrapped_mesh = sweep_local(wrapped_mesh, eastward[:, :, None, None], 1)
        wrapped_mesh = sweep_local(wrapped_mesh, northward[:, :, None, None], 0)
        wrapped_mesh = sweep_local(wrapped_mesh, eastward[None, None], 3)
        wrapped_mesh = sweep_local(wrapped_mesh, northward[None, None], 2)
    predicted_spread = wrapped_mesh.reshape(system_snapshots, system_snapshots)
    trace_entry_index = jnp.arange(system_snapshots, dtype=jnp.int32)
    predicted_spread = predicted_spread.at[trace_entry_index, trace_entry_index].add(process_noise_spread.reshape(system_snapshots))
    update_weighting = predicted_spread[:, sensor_targets]
    measured_entries = predicted_spread[sensor_targets, :]
    innovation = measured_entries[:, sensor_targets] + jnp.diag(noise_variance)
    factor = jnp.linalg.cholesky(innovation)
    inverse = jax.scipy.linalg.solve_triangular(factor, jnp.eye(OBS, dtype=jnp.float32), lower=True)
    lower_triangle_source = lax.dot_general(inverse, update_weighting, (((1,), (1,)), ((), ())), precision=finest_accuracy)
    lower_triangle_target = jnp.dot(inverse, measured_entries, precision=finest_accuracy)
    return predicted_spread - lax.dot_general(lower_triangle_source, lower_triangle_target, (((0,), (0,)), ((), ())), precision=finest_accuracy)
```

```python
import jax
import jax.numpy as jnp
from jax import lax
from jax.experimental import pallas as pl
from jax.experimental.pallas import tpu as pltpu
from jax.sharding import PartitionSpec as P

NC = 128
CYCLES = 2
TILE = 128
GROUP = 8


finest_accuracy = lax.Precision.HIGHEST


def from_everyone(array, axis):
    copies = jnp.broadcast_to(array, (lax.axis_size(axis), *array.shape))
    return lax.all_to_all(copies, axis, split_axis=0, concat_axis=0, tiled=True)


def from_neighbours(lower, upper, axis):
    size = lax.axis_size(axis)
    up = [(i, (i + 1) % size) for i in range(size)]
    down = [(j, i) for i, j in up]
    return lax.ppermute(upper, axis, up), lax.ppermute(lower, axis, down)


def stencil_weights(courant):
    return (
        courant * (1.0 + courant) * 0.5,
        1.0 - courant * courant,
        courant * (courant - 1.0) * 0.5,
    )


def sweep_local(field, courant, which_axis):
    weight_behind, weight_centre, weight_ahead = stencil_weights(courant)
    return (
        weight_behind * jnp.roll(field, 1, which_axis)
        + weight_centre * field
        + weight_ahead * jnp.roll(field, -1, which_axis)
    )


def sweep_padded(padded, courant, which_axis):
    keep = padded.shape[which_axis] - 2
    weight_behind, weight_centre, weight_ahead = stencil_weights(courant)
    return (
        weight_behind * lax.slice_in_dim(padded, 0, keep, axis=which_axis)
        + weight_centre * lax.slice_in_dim(padded, 1, keep + 1, axis=which_axis)
        + weight_ahead * lax.slice_in_dim(padded, 2, keep + 2, axis=which_axis)
    )


def wind_rows(courants, cycle, component, offset, length):
    surface = courants[cycle, component]
    doubled = jnp.concatenate([surface, surface], axis=0)
    return lax.dynamic_slice_in_dim(doubled, jnp.mod(offset, surface.shape[0]), length, 0)


def lane_spread(x, k):
    return jnp.broadcast_to(x[:, k : k + 1], x.shape)


def row_spread(x, k):
    return jnp.broadcast_to(x[k : k + 1, :], x.shape)


def tree_sum(terms):
    while len(terms) > 1:
        terms = [a + b for a, b in zip(terms[::2], terms[1::2])]
    return terms[0]


def inverse_tile(rows, lane, sub):
    rows = list(rows)
    for g in range(TILE // GROUP):
        panel = rows[g]
        first = GROUP * g
        inside = (lane >= first) & (lane < first + GROUP)
        cols = [lane_spread(panel, first + m) for m in range(GROUP)]
        for k in range(GROUP):
            here = sub == k
            flip = pl.reciprocal(row_spread(cols[k], k), approx=False)
            lead = cols[k]
            for m in range(GROUP):
                if m != k:
                    scaled = row_spread(cols[m], k) * flip
                    cols[m] = jnp.where(here, scaled, cols[m] - lead * scaled)
            cols[k] = jnp.where(here, flip, -lead * flip)
        panel = jnp.where(inside, jnp.where(lane - first == sub, 1.0, 0.0), panel)
        solved = tree_sum([cols[m] * row_spread(panel, m) for m in range(GROUP)])
        spread = [row_spread(solved, m) for m in range(GROUP)]
        for i in list(range(g + 1, len(rows))) + list(range(g)):
            change = tree_sum([lane_spread(rows[i], first + m) * spread[m] for m in range(GROUP)])
            rows[i] = jnp.where(inside, 0.0, rows[i]) - change
        rows[g] = solved
    return rows


def exact_dot(a, b):
    return jnp.dot(a, b, precision=finest_accuracy, preferred_element_type=jnp.float32)


def solve_kernel(innovation_ref, noise_ref, gain_ref, out_ref, work):
    size = innovation_ref.shape[0]
    lane = lax.broadcasted_iota(jnp.int32, (GROUP, TILE), 1)
    sub = lax.broadcasted_iota(jnp.int32, (GROUP, TILE), 0)
    square = innovation_ref[...]
    square = 0.5 * (square + square.T)
    diagonal = lax.broadcasted_iota(jnp.int32, (size, size), 0) == lax.broadcasted_iota(
        jnp.int32, (size, size), 1
    )
    work[:, :size] = jnp.where(diagonal, square + noise_ref[...], square)
    work[:, size:] = gain_ref[...]
    tiles = size // TILE
    for t in range(tiles):
        lo, hi = t * TILE, (t + 1) * TILE
        rows = [work[lo + GROUP * i : lo + GROUP * (i + 1), lo:hi] for i in range(TILE // GROUP)]
        inverse = jnp.concatenate(inverse_tile(rows, lane, sub), axis=0)
        solved = exact_dot(inverse, work[lo:hi, hi:])
        for i in range(tiles):
            if i != t:
                span = slice(i * TILE, (i + 1) * TILE)
                work[span, hi:] = work[span, hi:] - exact_dot(work[span, lo:hi], solved)
        work[lo:hi, hi:] = solved
    out_ref[...] = work[:, size:]


def solve_gain(innovation, noise, gain):
    return pl.pallas_call(
        solve_kernel,
        out_shape=jax.ShapeDtypeStruct(gain.shape, jnp.float32),
        in_specs=[pl.BlockSpec(memory_space=pltpu.VMEM)] * 3,
        out_specs=pl.BlockSpec(memory_space=pltpu.VMEM),
        scratch_shapes=[pltpu.VMEM((gain.shape[0], gain.shape[0] + gain.shape[1]), jnp.float32)],
        name="solve_gain",
    )(innovation, noise[None, :], gain)


def contract(a, b, dims):
    return lax.dot_general(a, b, (dims, ((), ())), precision=finest_accuracy)


def per_device(covariance, courants, process_noise_spread, sensor_targets, noise_variance):
    row_index = lax.axis_index("row")
    column_index = lax.axis_index("col")
    height, width = covariance.shape
    band_rows, band_columns = height // NC, width // NC
    row_first, column_first = row_index * band_rows, column_index * band_columns

    before, after = from_neighbours(
        covariance[: CYCLES * NC], covariance[height - CYCLES * NC :], "row"
    )
    field = jnp.concatenate([before, covariance, after], axis=0).reshape(-1, NC, width)
    for cycle in range(CYCLES):
        length = field.shape[0]
        offset = row_first - (CYCLES - cycle)
        field = sweep_local(field, wind_rows(courants, cycle, 0, offset, length)[:, :, None], 1)
        north = wind_rows(courants, cycle, 1, offset + 1, length - 2)[:, :, None]
        field = sweep_padded(field, north, 0)
    half_way = field.reshape(height, width)

    before, after = from_neighbours(
        half_way[:, : CYCLES * NC], half_way[:, width - CYCLES * NC :], "col"
    )
    field = jnp.concatenate([before, half_way, after], axis=1).reshape(height, -1, NC)
    for cycle in range(CYCLES):
        length = field.shape[1]
        offset = column_first - (CYCLES - cycle)
        field = sweep_local(field, wind_rows(courants, cycle, 0, offset, length)[None], 2)
        north = wind_rows(courants, cycle, 1, offset + 1, length - 2)[None]
        field = sweep_padded(field, north, 1)
    forecast = field.reshape(height, width)

    row_ids = row_index * height + jnp.arange(height, dtype=jnp.int32)
    column_ids = column_index * width + jnp.arange(width, dtype=jnp.int32)
    forecast = forecast + jnp.where(
        row_ids[:, None] == column_ids[None, :], process_noise_spread.reshape(height, 1), 0.0
    )

    sensors = sensor_targets.shape[0]
    row_share = sensors // lax.axis_size("row")
    column_share = sensors // lax.axis_size("col")
    row_sensors = lax.dynamic_slice_in_dim(sensor_targets, row_index * row_share, row_share)
    column_sensors = lax.dynamic_slice_in_dim(
        sensor_targets, column_index * column_share, column_share
    )
    pick_rows = (row_sensors[:, None] == row_ids[None, :]).astype(jnp.float32)
    pick_columns = (column_sensors[:, None] == column_ids[None, :]).astype(jnp.float32)

    gain = from_everyone(contract(pick_columns, forecast, ((1,), (1,))), "col")
    gain = gain.reshape(sensors, height)
    strip = contract(pick_rows, gain, ((1,), (1,)))
    innovation = from_everyone(strip, "row").reshape(sensors, sensors)
    obs_rows = from_everyone(contract(pick_rows, forecast, ((1,), (0,))), "row")
    obs_rows = obs_rows.reshape(sensors, width)
    solved = solve_gain(innovation, noise_variance, gain)
    return forecast - contract(solved, obs_rows, ((0,), (0,)))


def solution(mesh):
    in_specs = (P("row", "col"), P(), P("row", None), P(), P())
    out_specs = P("row", "col")
    return jax.shard_map(
        per_device, mesh=mesh, in_specs=in_specs, out_specs=out_specs, check_vma=False
    )
```

```python
import jax
import jax.numpy as jnp
from jax import lax
from jax.experimental import pallas as pl
from jax.experimental.pallas import tpu as pltpu
from jax.sharding import PartitionSpec as P

NC = 128
CYCLES = 2
TILE = 128
GROUP = 8


finest_accuracy = lax.Precision.HIGHEST


def from_everyone(array, axis):
    copies = jnp.broadcast_to(array, (lax.axis_size(axis), *array.shape))
    return lax.all_to_all(copies, axis, split_axis=0, concat_axis=0, tiled=True)


def from_neighbours(lower, upper, axis):
    size = lax.axis_size(axis)
    up = [(i, (i + 1) % size) for i in range(size)]
    down = [(j, i) for i, j in up]
    return lax.ppermute(upper, axis, up), lax.ppermute(lower, axis, down)


def stencil_weights(courant):
    return (
        courant * (1.0 + courant) * 0.5,
        1.0 - courant * courant,
        courant * (courant - 1.0) * 0.5,
    )


def sweep_local(field, courant, which_axis):
    weight_behind, weight_centre, weight_ahead = stencil_weights(courant)
    return (
        weight_behind * jnp.roll(field, 1, which_axis)
        + weight_centre * field
        + weight_ahead * jnp.roll(field, -1, which_axis)
    )


def sweep_padded(padded, courant, which_axis):
    keep = padded.shape[which_axis] - 2
    weight_behind, weight_centre, weight_ahead = stencil_weights(courant)
    return (
        weight_behind * lax.slice_in_dim(padded, 0, keep, axis=which_axis)
        + weight_centre * lax.slice_in_dim(padded, 1, keep + 1, axis=which_axis)
        + weight_ahead * lax.slice_in_dim(padded, 2, keep + 2, axis=which_axis)
    )


def wind_rows(courants, cycle, component, offset, length):
    surface = courants[cycle, component]
    doubled = jnp.concatenate([surface, surface], axis=0)
    return lax.dynamic_slice_in_dim(doubled, jnp.mod(offset, surface.shape[0]), length, 0)


def lane_spread(x, k):
    return jnp.broadcast_to(x[:, k : k + 1], x.shape)


def row_spread(x, k):
    return jnp.broadcast_to(x[k : k + 1, :], x.shape)


def tree_sum(terms):
    while len(terms) > 1:
        terms = [a + b for a, b in zip(terms[::2], terms[1::2])]
    return terms[0]


def inverse_tile(rows, lane, sub):
    rows = list(rows)
    for g in range(TILE // GROUP):
        panel = rows[g]
        first = GROUP * g
        inside = (lane >= first) & (lane < first + GROUP)
        cols = [lane_spread(panel, first + m) for m in range(GROUP)]
        for k in range(GROUP):
            here = sub == k
            flip = pl.reciprocal(row_spread(cols[k], k), approx=False)
            lead = cols[k]
            for m in range(GROUP):
                if m != k:
                    scaled = row_spread(cols[m], k) * flip
                    cols[m] = jnp.where(here, scaled, cols[m] - lead * scaled)
            cols[k] = jnp.where(here, flip, -lead * flip)
        panel = jnp.where(inside, jnp.where(lane - first == sub, 1.0, 0.0), panel)
        solved = tree_sum([cols[m] * row_spread(panel, m) for m in range(GROUP)])
        spread = [row_spread(solved, m) for m in range(GROUP)]
        for i in list(range(g + 1, len(rows))) + list(range(g)):
            change = tree_sum([lane_spread(rows[i], first + m) * spread[m] for m in range(GROUP)])
            rows[i] = jnp.where(inside, 0.0, rows[i]) - change
        rows[g] = solved
    return rows


def exact_dot(a, b):
    return jnp.dot(a, b, precision=finest_accuracy, preferred_element_type=jnp.float32)


def inverse_kernel(innovation_ref, noise_ref, out_ref):
    size = innovation_ref.shape[0]
    lane = lax.broadcasted_iota(jnp.int32, (GROUP, TILE), 1)
    sub = lax.broadcasted_iota(jnp.int32, (GROUP, TILE), 0)
    square = innovation_ref[...]
    square = 0.5 * (square + square.T)
    diagonal = lax.broadcasted_iota(jnp.int32, (size, size), 0) == lax.broadcasted_iota(
        jnp.int32, (size, size), 1
    )
    out_ref[...] = jnp.where(diagonal, square + noise_ref[...], square)
    tiles = size // TILE
    unit = jnp.where(
        lax.broadcasted_iota(jnp.int32, (TILE, TILE), 0)
        == lax.broadcasted_iota(jnp.int32, (TILE, TILE), 1),
        1.0,
        0.0,
    )

    def eliminate(t, carry):
        start = pl.multiple_of(t * TILE, TILE)
        here = pl.ds(start, TILE)
        rows = [
            out_ref[pl.ds(pl.multiple_of(start + GROUP * i, GROUP), GROUP), here]
            for i in range(TILE // GROUP)
        ]
        inverse = jnp.concatenate(inverse_tile(rows, lane, sub), axis=0)
        out_ref[here, here] = unit
        solved = exact_dot(inverse, out_ref[here, :])
        out_ref[here, :] = solved
        for other in range(1, tiles):
            there = pl.ds(pl.multiple_of(lax.rem(t + other, tiles) * TILE, TILE), TILE)
            column = out_ref[there, here]
            out_ref[there, here] = jnp.zeros((TILE, TILE), jnp.float32)
            out_ref[there, :] = out_ref[there, :] - exact_dot(column, solved)
        return carry

    lax.fori_loop(0, tiles, eliminate, 0)


def inverse_of(innovation, noise):
    return pl.pallas_call(
        inverse_kernel,
        out_shape=jax.ShapeDtypeStruct(innovation.shape, jnp.float32),
        in_specs=[pl.BlockSpec(memory_space=pltpu.VMEM)] * 2,
        out_specs=pl.BlockSpec(memory_space=pltpu.VMEM),
        name="inverse_of",
    )(innovation, noise[None, :])


def contract(a, b, dims):
    return lax.dot_general(a, b, (dims, ((), ())), precision=finest_accuracy)


def step_rows(field, courants, cycle, first):
    length = field.shape[0]
    field = sweep_local(field, wind_rows(courants, cycle, 0, first, length)[:, :, None], 1)
    north = wind_rows(courants, cycle, 1, first + 1, length - 2)[:, :, None]
    return sweep_padded(field, north, 0)


def step_columns(field, courants, cycle, first):
    length = field.shape[1]
    field = sweep_local(field, wind_rows(courants, cycle, 0, first, length)[None], 2)
    north = wind_rows(courants, cycle, 1, first + 1, length - 2)[None]
    return sweep_padded(field, north, 1)


def forecast_weights(targets, courants, first, length):
    cells = courants.shape[2] * NC
    span = length + 2 * CYCLES
    place = jnp.mod(targets - (first - CYCLES) * NC, cells)
    grid = lax.broadcasted_iota(jnp.int32, (1, span, NC), 1) * NC + lax.broadcasted_iota(
        jnp.int32, (1, span, NC), 2
    )
    weights = (place[:, None, None] == grid).astype(jnp.float32)
    for cycle in reversed(range(CYCLES)):
        size = weights.shape[1]
        origin = first - cycle - 1
        north = wind_rows(courants, cycle, 1, origin, size)[None]
        behind, centre, ahead = [w * weights for w in stencil_weights(north)]
        weights = behind[:, 2:] + centre[:, 1 : size - 1] + ahead[:, : size - 2]
        east = wind_rows(courants, cycle, 0, origin + 1, size - 2)[None]
        behind, centre, ahead = [w * weights for w in stencil_weights(east)]
        weights = jnp.roll(behind, -1, 2) + centre + jnp.roll(ahead, 1, 2)
    return weights.reshape(targets.shape[0], length * NC)


def three_bands(targets, band, share):
    doubled = jnp.concatenate([targets, targets])
    start = jnp.mod((band - 1) * share, targets.shape[0])
    return lax.dynamic_slice_in_dim(doubled, start, 3 * share)


def by_shifts(part, axis):
    size, mine = lax.axis_size(axis), lax.axis_index(axis)
    parts = jnp.zeros((size, *part.shape), part.dtype)
    parts = lax.dynamic_update_index_in_dim(parts, part, mine, 0)
    for shift in range(1, size):
        got = lax.ppermute(part, axis, [(i, (i + shift) % size) for i in range(size)])
        parts = lax.dynamic_update_index_in_dim(parts, got, jnp.mod(mine - shift, size), 0)
    return parts


def sum_of_bands(shares, axis):
    share = shares.shape[0] // 3
    from_below, from_above = from_neighbours(shares[:share], shares[2 * share :], axis)
    return shares[share : 2 * share] + from_below + from_above


def step_narrow(tile, courants, first, axis):
    edge, length = CYCLES * NC, tile.shape[1]
    before, after = from_neighbours(tile[:, :edge], tile[:, length - edge :], axis)
    field = jnp.concatenate([before, tile, after], axis=1).reshape(tile.shape[0], -1, NC)
    for cycle in range(CYCLES):
        field = step_columns(field, courants, cycle, first - CYCLES + cycle)
    return field.reshape(tile.shape)


def per_device(covariance, courants, process_noise_spread, sensor_targets, noise_variance):
    row_index, column_index = lax.axis_index(ROW), lax.axis_index(COL)
    height, width = covariance.shape
    band_rows, band_columns = height // NC, width // NC
    row_first, column_first = row_index * band_rows, column_index * band_columns
    edge = CYCLES * NC
    sensors = sensor_targets.shape[0]
    row_share = sensors // lax.axis_size(ROW)
    column_share = sensors // lax.axis_size(COL)
    row_targets = three_bands(sensor_targets, row_index, row_share)
    column_targets = three_bands(sensor_targets, column_index, column_share)
    row_sensors = row_targets[row_share : 2 * row_share]
    column_sensors = column_targets[column_share : 2 * column_share]
    row_ids = row_index * height + jnp.arange(height, dtype=jnp.int32)
    column_ids = column_index * width + jnp.arange(width, dtype=jnp.int32)
    noise_here = process_noise_spread.reshape(height, 1)
    pick_rows = row_sensors[:, None] == row_ids[None, :]
    pick_columns = column_sensors[:, None] == column_ids[None, :]
    row_noise = jnp.sum(jnp.where(pick_rows, noise_here[:, 0][None, :], 0.0), axis=1)

    with jax.named_scope("tiles"):
        row_weights = forecast_weights(row_targets, courants, row_first, band_rows)
        column_weights = forecast_weights(column_targets, courants, column_first, band_columns)
        obs = sum_of_bands(contract(row_weights, covariance, ((1,), (0,))), ROW)
        gain = sum_of_bands(contract(column_weights, covariance, ((1,), (1,))), COL)
        obs = step_narrow(obs, courants, column_first, COL)
        gain = step_narrow(gain, courants, row_first, ROW)
        obs = obs + jnp.where(
            row_sensors[:, None] == column_ids[None, :], row_noise[:, None], 0.0
        )
        gain = gain + jnp.where(
            column_sensors[:, None] == row_ids[None, :], noise_here[:, 0][None, :], 0.0
        )
        block = contract(obs, pick_columns.astype(jnp.float32), ((1,), (1,)))

    high = lax.axis_size("zh")
    with jax.named_scope("innovation"):
        block = from_everyone(block.reshape(-1, NC), ("y", "zl", "zh"))
        block, covariance, obs, gain = lax.optimization_barrier((block, covariance, obs, gain))
        block = block.reshape(-1, high, row_share, column_share)
        slab = block.transpose(1, 3, 0, 2).reshape(high * column_share, sensors)
        slabs = from_everyone(slab, ("x", "core"))
        flat = (lax.axis_size("x"), lax.axis_size("core"), high, column_share, sensors)
        innovation = slabs.reshape(flat).transpose(0, 2, 1, 3, 4).reshape(sensors, sensors)

    with jax.named_scope("forecast"):
        before, after = from_neighbours(covariance[:edge], covariance[height - edge :], ROW)
        field = jnp.concatenate([before, covariance, after], axis=0).reshape(-1, NC, width)
        for cycle in range(CYCLES):
            field = step_rows(field, courants, cycle, row_first - CYCLES + cycle)
        half_way = field.reshape(height, width)
        innovation, half_way = lax.optimization_barrier((innovation, half_way))
        before, after = from_neighbours(half_way[:, :edge], half_way[:, width - edge :], COL)
        inverse = inverse_of(innovation, noise_variance)

    with jax.named_scope("gathers"):
        obs_rows = by_shifts(obs, "zl").reshape(-1, width)
        gain = by_shifts(by_shifts(gain, "core"), "zh").reshape(-1, *gain.shape)
        gain = gain.reshape(-1, height)
        gain = by_shifts(gain, "x").reshape(sensors, height)
        obs_rows = from_everyone(obs_rows, "y").reshape(sensors, width)
        solved = contract(inverse, gain, ((1,), (0,)))

    with jax.named_scope("forecast_end"):
        field = jnp.concatenate([before, half_way, after], axis=1).reshape(height, -1, NC)
        for cycle in range(CYCLES):
            field = step_columns(field, courants, cycle, column_first - CYCLES + cycle)
        forecast = field.reshape(height, width) + jnp.where(
            row_ids[:, None] == column_ids[None, :], noise_here, 0.0
        )
    return forecast - contract(solved, obs_rows, ((0,), (0,)))


ROW = ("y", "zl")
COL = ("x", "zh", "core")


def physical(mesh):
    rows, columns = mesh.devices.shape
    zl, zh, core = 4, 2, 2
    shape = (rows // zl, zl, columns // (zh * core), zh, core)
    return jax.sharding.Mesh(mesh.devices.reshape(shape), ROW + COL)


def solution(mesh):
    in_specs = (P(ROW, COL), P(), P(ROW, None), P(), P())
    out_specs = P(ROW, COL)
    return jax.shard_map(
        per_device, mesh=physical(mesh), in_specs=in_specs, out_specs=out_specs, check_vma=False
    )
```

```python
import jax
import jax.numpy as jnp
from jax import lax
from jax.experimental import pallas as pl
from jax.experimental.pallas import tpu as pltpu
from jax.sharding import PartitionSpec as P

NC = 128
CYCLES = 2
TILE = 128
GROUP = 8


finest_accuracy = lax.Precision.HIGHEST


def from_everyone(array, axis):
    copies = jnp.broadcast_to(array, (lax.axis_size(axis), *array.shape))
    return lax.all_to_all(copies, axis, split_axis=0, concat_axis=0, tiled=True)


def from_neighbours(lower, upper, axis):
    size = lax.axis_size(axis)
    up = [(i, (i + 1) % size) for i in range(size)]
    down = [(j, i) for i, j in up]
    return lax.ppermute(upper, axis, up), lax.ppermute(lower, axis, down)


def stencil_weights(courant):
    return (
        courant * (1.0 + courant) * 0.5,
        1.0 - courant * courant,
        courant * (courant - 1.0) * 0.5,
    )


def sweep_local(field, courant, which_axis):
    weight_behind, weight_centre, weight_ahead = stencil_weights(courant)
    return (
        weight_behind * jnp.roll(field, 1, which_axis)
        + weight_centre * field
        + weight_ahead * jnp.roll(field, -1, which_axis)
    )


def sweep_padded(padded, courant, which_axis):
    keep = padded.shape[which_axis] - 2
    weight_behind, weight_centre, weight_ahead = stencil_weights(courant)
    return (
        weight_behind * lax.slice_in_dim(padded, 0, keep, axis=which_axis)
        + weight_centre * lax.slice_in_dim(padded, 1, keep + 1, axis=which_axis)
        + weight_ahead * lax.slice_in_dim(padded, 2, keep + 2, axis=which_axis)
    )


def wind_rows(courants, cycle, component, offset, length):
    surface = courants[cycle, component]
    doubled = jnp.concatenate([surface, surface], axis=0)
    return lax.dynamic_slice_in_dim(doubled, jnp.mod(offset, surface.shape[0]), length, 0)


def lane_spread(x, k):
    return jnp.broadcast_to(x[:, k : k + 1], x.shape)


def row_spread(x, k):
    return jnp.broadcast_to(x[k : k + 1, :], x.shape)


def tree_sum(terms):
    while len(terms) > 1:
        terms = [a + b for a, b in zip(terms[::2], terms[1::2])]
    return terms[0]


def inverse_tile(rows, lane, sub):
    rows = list(rows)
    for g in range(TILE // GROUP):
        panel = rows[g]
        first = GROUP * g
        inside = (lane >= first) & (lane < first + GROUP)
        cols = [lane_spread(panel, first + m) for m in range(GROUP)]
        for k in range(GROUP):
            here = sub == k
            flip = pl.reciprocal(row_spread(cols[k], k), approx=False)
            lead = cols[k]
            for m in range(GROUP):
                if m != k:
                    scaled = row_spread(cols[m], k) * flip
                    cols[m] = jnp.where(here, scaled, cols[m] - lead * scaled)
            cols[k] = jnp.where(here, flip, -lead * flip)
        panel = jnp.where(inside, jnp.where(lane - first == sub, 1.0, 0.0), panel)
        solved = tree_sum([cols[m] * row_spread(panel, m) for m in range(GROUP)])
        spread = [row_spread(solved, m) for m in range(GROUP)]
        for i in list(range(g + 1, len(rows))) + list(range(g)):
            change = tree_sum([lane_spread(rows[i], first + m) * spread[m] for m in range(GROUP)])
            rows[i] = jnp.where(inside, 0.0, rows[i]) - change
        rows[g] = solved
    return rows


def exact_dot(a, b):
    return jnp.dot(a, b, precision=finest_accuracy, preferred_element_type=jnp.float32)


def inverse_kernel(innovation_ref, noise_ref, out_ref):
    size = innovation_ref.shape[0]
    lane = lax.broadcasted_iota(jnp.int32, (GROUP, TILE), 1)
    sub = lax.broadcasted_iota(jnp.int32, (GROUP, TILE), 0)
    square = innovation_ref[...]
    square = 0.5 * (square + square.T)
    diagonal = lax.broadcasted_iota(jnp.int32, (size, size), 0) == lax.broadcasted_iota(
        jnp.int32, (size, size), 1
    )
    out_ref[...] = jnp.where(diagonal, square + noise_ref[...], square)
    tiles = size // TILE
    spans = [slice(t * TILE, (t + 1) * TILE) for t in range(tiles)]
    for t in range(tiles):
        here = spans[t]
        rows = [
            out_ref[t * TILE + GROUP * i : t * TILE + GROUP * (i + 1), here]
            for i in range(TILE // GROUP)
        ]
        inverse = jnp.concatenate(inverse_tile(rows, lane, sub), axis=0)
        for j in range(tiles):
            if j != t:
                out_ref[here, spans[j]] = exact_dot(inverse, out_ref[here, spans[j]])
        for i in range(tiles):
            if i != t:
                column = out_ref[spans[i], here]
                for j in range(tiles):
                    if j != t:
                        out_ref[spans[i], spans[j]] = out_ref[spans[i], spans[j]] - exact_dot(
                            column, out_ref[here, spans[j]]
                        )
                out_ref[spans[i], here] = -exact_dot(column, inverse)
        out_ref[here, here] = inverse


def inverse_of(innovation, noise):
    return pl.pallas_call(
        inverse_kernel,
        out_shape=jax.ShapeDtypeStruct(innovation.shape, jnp.float32),
        in_specs=[pl.BlockSpec(memory_space=pltpu.VMEM)] * 2,
        out_specs=pl.BlockSpec(memory_space=pltpu.VMEM),
        name="inverse_of",
    )(innovation, noise[None, :])


def contract(a, b, dims):
    return lax.dot_general(a, b, (dims, ((), ())), precision=finest_accuracy)


def step_rows(field, courants, cycle, first):
    length = field.shape[0]
    field = sweep_local(field, wind_rows(courants, cycle, 0, first, length)[:, :, None], 1)
    north = wind_rows(courants, cycle, 1, first + 1, length - 2)[:, :, None]
    return sweep_padded(field, north, 0)


def step_columns(field, courants, cycle, first):
    length = field.shape[1]
    field = sweep_local(field, wind_rows(courants, cycle, 0, first, length)[None], 2)
    north = wind_rows(courants, cycle, 1, first + 1, length - 2)[None]
    return sweep_padded(field, north, 1)


def by_shifts(part, axis):
    size, mine = lax.axis_size(axis), lax.axis_index(axis)
    parts = jnp.zeros((size, *part.shape), part.dtype)
    parts = lax.dynamic_update_index_in_dim(parts, part, mine, 0)
    for shift in range(1, size):
        got = lax.ppermute(part, axis, [(i, (i + shift) % size) for i in range(size)])
        parts = lax.dynamic_update_index_in_dim(parts, got, jnp.mod(mine - shift, size), 0)
    return parts


def one_cycle(covariance, courants, process_noise_spread, sensor_targets, noise_variance):
    row_index, column_index = lax.axis_index(ROW), lax.axis_index(COL)
    height, width = covariance.shape
    band_rows, band_columns = height // NC, width // NC
    row_first, column_first = row_index * band_rows, column_index * band_columns
    edge = CYCLES * NC

    before, after = from_neighbours(covariance[:edge], covariance[height - edge :], ROW)
    field = jnp.concatenate([before, covariance, after], axis=0).reshape(-1, NC, width)
    for cycle in range(CYCLES):
        field = step_rows(field, courants, cycle, row_first - CYCLES + cycle)
    half_way = field.reshape(height, width)

    before, after = from_neighbours(half_way[:, :edge], half_way[:, width - edge :], COL)
    field = jnp.concatenate([before, half_way, after], axis=1).reshape(height, -1, NC)
    for cycle in range(CYCLES):
        field = step_columns(field, courants, cycle, column_first - CYCLES + cycle)
    forecast = field.reshape(height, width)

    row_ids = row_index * height + jnp.arange(height, dtype=jnp.int32)
    column_ids = column_index * width + jnp.arange(width, dtype=jnp.int32)
    forecast = forecast + jnp.where(
        row_ids[:, None] == column_ids[None, :], process_noise_spread.reshape(height, 1), 0.0
    )

    sensors = sensor_targets.shape[0]
    row_share = sensors // lax.axis_size(ROW)
    column_share = sensors // lax.axis_size(COL)
    row_sensors = lax.dynamic_slice_in_dim(sensor_targets, row_index * row_share, row_share)
    column_sensors = lax.dynamic_slice_in_dim(
        sensor_targets, column_index * column_share, column_share
    )
    pick_rows = (row_sensors[:, None] == row_ids[None, :]).astype(jnp.float32)
    pick_columns = (column_sensors[:, None] == column_ids[None, :]).astype(jnp.float32)
    obs = contract(pick_rows, forecast, ((1,), (0,)))
    block = contract(obs, pick_columns, ((1,), (1,)))
    gain = contract(pick_columns, forecast, ((1,), (1,)))

    high = lax.axis_size("zh")
    block = from_everyone(block.reshape(-1, NC), ("y", "zl", "zh"))
    gain = by_shifts(by_shifts(gain, "core"), "zh").reshape(-1, height)
    block, gain, obs = lax.optimization_barrier((block, gain, obs))
    block = block.reshape(-1, high, row_share, column_share)
    slab = block.transpose(1, 3, 0, 2).reshape(high * column_share, sensors)
    slabs = from_everyone(slab, ("x", "core"))
    flat = (lax.axis_size("x"), lax.axis_size("core"), high, column_share, sensors)
    innovation = slabs.reshape(flat).transpose(0, 2, 1, 3, 4).reshape(sensors, sensors)

    gain = by_shifts(gain, "x").reshape(sensors, height)
    innovation, gain, obs = lax.optimization_barrier((innovation, gain, obs))
    obs_rows = from_everyone(obs, ROW).reshape(sensors, width)
    solved = contract(inverse_of(innovation, noise_variance), gain, ((1,), (0,)))
    return forecast - contract(solved, obs_rows, ((0,), (0,)))


ROW = ("y", "zl")
COL = ("x", "zh", "core")


def physical(mesh):
    rows, columns = mesh.devices.shape
    zl, zh, core = 4, 2, 2
    shape = (rows // zl, zl, columns // (zh * core), zh, core)
    return jax.sharding.Mesh(mesh.devices.reshape(shape), ROW + COL)


def solution(mesh):
    in_specs = (P(ROW, COL), P(), P(ROW, None), P(), P())
    out_specs = P(ROW, COL)
    return jax.shard_map(
        one_cycle, mesh=physical(mesh), in_specs=in_specs, out_specs=out_specs, check_vma=False
    )
```

```python
import jax
import jax.numpy as jnp
from jax import lax
from jax.experimental import pallas as pl
from jax.experimental.pallas import tpu as pltpu
from jax.sharding import PartitionSpec as P

NC = 128
CYCLES = 2
TILE = 128
GROUP = 8
STRIP = 32
CORES = 2
HALVES = 2


finest_accuracy = lax.Precision.HIGHEST


def from_everyone(array, axis):
    copies = jnp.broadcast_to(array, (lax.axis_size(axis), *array.shape))
    return lax.all_to_all(copies, axis, split_axis=0, concat_axis=0, tiled=True)


def from_neighbours(lower, upper, axis):
    size = lax.axis_size(axis)
    up = [(i, (i + 1) % size) for i in range(size)]
    down = [(j, i) for i, j in up]
    return lax.ppermute(upper, axis, up), lax.ppermute(lower, axis, down)


def stencil_weights(courant):
    return (
        courant * (1.0 + courant) * 0.5,
        1.0 - courant * courant,
        courant * (courant - 1.0) * 0.5,
    )


def sweep_local(field, courant, which_axis):
    weight_behind, weight_centre, weight_ahead = stencil_weights(courant)
    return (
        weight_behind * jnp.roll(field, 1, which_axis)
        + weight_centre * field
        + weight_ahead * jnp.roll(field, -1, which_axis)
    )


def sweep_padded(padded, courant, which_axis):
    keep = padded.shape[which_axis] - 2
    weight_behind, weight_centre, weight_ahead = stencil_weights(courant)
    return (
        weight_behind * lax.slice_in_dim(padded, 0, keep, axis=which_axis)
        + weight_centre * lax.slice_in_dim(padded, 1, keep + 1, axis=which_axis)
        + weight_ahead * lax.slice_in_dim(padded, 2, keep + 2, axis=which_axis)
    )


def wind_rows(courants, cycle, component, offset, length):
    surface = courants[cycle, component]
    doubled = jnp.concatenate([surface, surface], axis=0)
    return lax.dynamic_slice_in_dim(doubled, jnp.mod(offset, surface.shape[0]), length, 0)


def lane_spread(x, k):
    return jnp.broadcast_to(x[:, k : k + 1], x.shape)


def row_spread(x, k):
    return jnp.broadcast_to(x[k : k + 1, :], x.shape)


def tree_sum(terms):
    while len(terms) > 1:
        terms = [a + b for a, b in zip(terms[::2], terms[1::2])]
    return terms[0]


def inverse_tile(rows, lane, sub):
    rows = list(rows)
    for g in range(TILE // GROUP):
        panel = rows[g]
        first = GROUP * g
        inside = (lane >= first) & (lane < first + GROUP)
        cols = [lane_spread(panel, first + m) for m in range(GROUP)]
        for k in range(GROUP):
            here = sub == k
            flip = pl.reciprocal(row_spread(cols[k], k), approx=False)
            lead = cols[k]
            for m in range(GROUP):
                if m != k:
                    scaled = row_spread(cols[m], k) * flip
                    cols[m] = jnp.where(here, scaled, cols[m] - lead * scaled)
            cols[k] = jnp.where(here, flip, -lead * flip)
        panel = jnp.where(inside, jnp.where(lane - first == sub, 1.0, 0.0), panel)
        solved = tree_sum([cols[m] * row_spread(panel, m) for m in range(GROUP)])
        spread = [row_spread(solved, m) for m in range(GROUP)]
        for i in list(range(g + 1, len(rows))) + list(range(g)):
            change = tree_sum([lane_spread(rows[i], first + m) * spread[m] for m in range(GROUP)])
            rows[i] = jnp.where(inside, 0.0, rows[i]) - change
        rows[g] = solved
    return rows


def exact_dot(a, b):
    return jnp.dot(a, b, precision=finest_accuracy, preferred_element_type=jnp.float32)


def solve_kernel(slabs_ref, noise_ref, out_ref, work):
    size = noise_ref.shape[1]
    lane = lax.broadcasted_iota(jnp.int32, (GROUP, TILE), 1)
    sub = lax.broadcasted_iota(jnp.int32, (GROUP, TILE), 0)
    slabs, share = slabs_ref.shape[0], slabs_ref.shape[1] // HALVES
    for n in range(slabs):
        for half in range(HALVES):
            place = (n // CORES * HALVES + half) * CORES + n % CORES
            work[place * share : (place + 1) * share, :] = slabs_ref[
                n, half * share : (half + 1) * share, :
            ]
    square = work[:, :size]
    square = 0.5 * (square + square.T)
    diagonal = lax.broadcasted_iota(jnp.int32, (size, size), 0) == lax.broadcasted_iota(
        jnp.int32, (size, size), 1
    )
    work[:, :size] = jnp.where(diagonal, square + noise_ref[...], square)
    tiles = size // TILE
    for t in range(tiles):
        lo, hi = t * TILE, (t + 1) * TILE
        rows = [work[lo + GROUP * i : lo + GROUP * (i + 1), lo:hi] for i in range(TILE // GROUP)]
        inverse = jnp.concatenate(inverse_tile(rows, lane, sub), axis=0)
        solved = exact_dot(inverse, work[lo:hi, hi:])
        for i in range(tiles):
            if i != t:
                span = slice(i * TILE, (i + 1) * TILE)
                work[span, hi:] = work[span, hi:] - exact_dot(work[span, lo:hi], solved)
        work[lo:hi, hi:] = solved
    out_ref[...] = work[:, size:]


def solve_gain(slabs, noise):
    size, wide = noise.shape[0], slabs.shape[2]
    return pl.pallas_call(
        solve_kernel,
        out_shape=jax.ShapeDtypeStruct((size, wide - size), jnp.float32),
        in_specs=[pl.BlockSpec(memory_space=pltpu.VMEM)] * 2,
        out_specs=pl.BlockSpec(memory_space=pltpu.VMEM),
        scratch_shapes=[pltpu.VMEM((size, wide), jnp.float32)],
        name="solve_gain",
    )(slabs, noise[None, :])


def columns_kernel(*refs):
    fields, winds, (noise_ref, shift_ref, out_ref) = refs[:4], refs[4:8], refs[8:]
    height = out_ref.shape[0]
    for start in range(0, height, STRIP):
        strip = slice(start, start + STRIP)
        tiles = [
            ref[strip, k * NC : (k + 1) * NC]
            for ref in fields
            for k in range(ref.shape[1] // NC)
        ]
        for cycle in range(CYCLES):
            east, north = winds[2 * cycle][...], winds[2 * cycle + 1][...]
            behind, centre, ahead = stencil_weights(east)
            tiles = [
                behind[i : i + 1] * pltpu.roll(tile, 1, 1)
                + centre[i : i + 1] * tile
                + ahead[i : i + 1] * pltpu.roll(tile, NC - 1, 1)
                for i, tile in enumerate(tiles)
            ]
            behind, centre, ahead = stencil_weights(north)
            tiles = [
                behind[i : i + 1] * tiles[i]
                + centre[i : i + 1] * tiles[i + 1]
                + ahead[i : i + 1] * tiles[i + 2]
                for i in range(len(tiles) - 2)
            ]
        row = lax.broadcasted_iota(jnp.int32, (STRIP, NC), 0) + (shift_ref[0] + start)
        column = lax.broadcasted_iota(jnp.int32, (STRIP, NC), 1)
        for i, tile in enumerate(tiles):
            here = slice(i * NC, (i + 1) * NC)
            out_ref[strip, here] = tile + jnp.where(
                row == column + i * NC, noise_ref[:, here], 0.0
            )


def columns_forecast(fields, winds, noise, shift):
    height = fields[0].shape[0]
    return pl.pallas_call(
        columns_kernel,
        out_shape=jax.ShapeDtypeStruct((height, noise.shape[1]), jnp.float32),
        in_specs=[pl.BlockSpec(memory_space=pltpu.VMEM)] * 9
        + [pl.BlockSpec(memory_space=pltpu.SMEM)],
        out_specs=pl.BlockSpec(memory_space=pltpu.VMEM),
        name="columns_forecast",
    )(*fields, *winds, noise, shift)


def contract(a, b, dims):
    return lax.dot_general(a, b, (dims, ((), ())), precision=finest_accuracy)


def step_rows(field, courants, cycle, first):
    length = field.shape[0]
    field = sweep_local(field, wind_rows(courants, cycle, 0, first, length)[:, :, None], 1)
    north = wind_rows(courants, cycle, 1, first + 1, length - 2)[:, :, None]
    return sweep_padded(field, north, 0)


def by_shifts(part, axis):
    size, mine = lax.axis_size(axis), lax.axis_index(axis)
    parts = jnp.zeros((size, *part.shape), part.dtype)
    parts = lax.dynamic_update_index_in_dim(parts, part, mine, 0)
    for shift in range(1, size):
        got = lax.ppermute(part, axis, [(i, (i + shift) % size) for i in range(size)])
        parts = lax.dynamic_update_index_in_dim(parts, got, jnp.mod(mine - shift, size), 0)
    return parts


def one_cycle(covariance, courants, process_noise_spread, sensor_targets, noise_variance):
    row_index, column_index = lax.axis_index(ROW), lax.axis_index(COL)
    height, width = covariance.shape
    band_rows, band_columns = height // NC, width // NC
    row_first, column_first = row_index * band_rows, column_index * band_columns
    edge = CYCLES * NC

    halves = []
    for part in (covariance[:, width - edge :], covariance[:, :edge]):
        before, after = from_neighbours(part[:edge], part[height - edge :], ROW)
        if halves:
            before, after, _ = lax.optimization_barrier((before, after, halves[0]))
        field = jnp.concatenate([before, part, after], axis=0).reshape(-1, NC, edge)
        for cycle in range(CYCLES):
            field = step_rows(field, courants, cycle, row_first - CYCLES + cycle)
        halves.append(field.reshape(height, edge))
    upper, lower = halves
    before, after = from_neighbours(lower, upper, COL)
    winds = []
    for cycle in range(CYCLES):
        first, length = column_first - CYCLES + cycle, band_columns + 2 * (CYCLES - cycle)
        winds.append(wind_rows(courants, cycle, 0, first, length))
        winds.append(wind_rows(courants, cycle, 1, first + 1, length - 2))
    noise_here = process_noise_spread.reshape(1, height)
    offset = row_first - column_first
    noise_columns = jnp.concatenate(
        [jnp.where(offset == k, noise_here, 0.0) for k in range(0, band_columns, band_rows)], axis=1
    )
    forecast = columns_forecast(
        (before, lower, upper, after), winds, noise_columns, jnp.reshape(offset * NC, (1,))
    )
    row_ids = row_index * height + jnp.arange(height, dtype=jnp.int32)
    column_ids = column_index * width + jnp.arange(width, dtype=jnp.int32)

    sensors = sensor_targets.shape[0]
    row_share = sensors // lax.axis_size(ROW)
    column_share = sensors // lax.axis_size(COL)
    row_sensors = lax.dynamic_slice_in_dim(sensor_targets, row_index * row_share, row_share)
    column_sensors = lax.dynamic_slice_in_dim(
        sensor_targets, column_index * column_share, column_share
    )
    pick_rows = (row_sensors[:, None] == row_ids[None, :]).astype(jnp.float32)
    pick_columns = (column_sensors[:, None] == column_ids[None, :]).astype(jnp.float32)
    obs = contract(pick_rows, forecast, ((1,), (0,)))
    block = contract(obs, pick_columns, ((1,), (1,)))
    gain = contract(pick_columns, forecast, ((1,), (1,)))

    high = lax.axis_size("zh")
    block = from_everyone(block.reshape(-1, NC), ("y", "zl", "zh"))
    gain = by_shifts(gain, "zh").reshape(-1, height)
    block, gain, obs = lax.optimization_barrier((block, gain, obs))
    block = block.reshape(-1, high, row_share, column_share)
    slab = block.transpose(1, 3, 0, 2).reshape(high * column_share, sensors)
    slabs = from_everyone(jnp.concatenate([slab, gain], axis=1), ("x", "core"))
    slabs, obs = lax.optimization_barrier((slabs, obs))

    obs_rows = from_everyone(obs, ROW).reshape(sensors, width)
    solved = solve_gain(slabs, noise_variance)
    return forecast - contract(solved, obs_rows, ((0,), (0,)))


ROW = ("y", "zl")
COL = ("x", "zh", "core")


def physical(mesh):
    rows, columns = mesh.devices.shape
    zl, zh, core = 4, HALVES, CORES
    shape = (rows // zl, zl, columns // (zh * core), zh, core)
    return jax.sharding.Mesh(mesh.devices.reshape(shape), ROW + COL)


def solution(mesh):
    in_specs = (P(ROW, COL), P(), P(ROW, None), P(), P())
    out_specs = P(ROW, COL)
    return jax.shard_map(
        one_cycle, mesh=physical(mesh), in_specs=in_specs, out_specs=out_specs, check_vma=False
    )
```

```python
import jax
import jax.numpy as jnp
from jax import lax
from jax.experimental import pallas as pl
from jax.experimental.pallas import tpu as pltpu
from jax.sharding import PartitionSpec as P

NC = 128
CYCLES = 2
TILE = 128
GROUP = 8
STRIP = 64
CORES = 2
HALVES = 2


finest_accuracy = lax.Precision.HIGHEST


def from_everyone(array, axis):
    copies = jnp.broadcast_to(array, (lax.axis_size(axis), *array.shape))
    return lax.all_to_all(copies, axis, split_axis=0, concat_axis=0, tiled=True)


def from_neighbours(lower, upper, axis):
    size = lax.axis_size(axis)
    up = [(i, (i + 1) % size) for i in range(size)]
    down = [(j, i) for i, j in up]
    return lax.ppermute(upper, axis, up), lax.ppermute(lower, axis, down)


def stencil_weights(courant):
    return (
        courant * (1.0 + courant) * 0.5,
        1.0 - courant * courant,
        courant * (courant - 1.0) * 0.5,
    )


def sweep_local(field, courant, which_axis):
    weight_behind, weight_centre, weight_ahead = stencil_weights(courant)
    return (
        weight_behind * jnp.roll(field, 1, which_axis)
        + weight_centre * field
        + weight_ahead * jnp.roll(field, -1, which_axis)
    )


def sweep_padded(padded, courant, which_axis):
    keep = padded.shape[which_axis] - 2
    weight_behind, weight_centre, weight_ahead = stencil_weights(courant)
    return (
        weight_behind * lax.slice_in_dim(padded, 0, keep, axis=which_axis)
        + weight_centre * lax.slice_in_dim(padded, 1, keep + 1, axis=which_axis)
        + weight_ahead * lax.slice_in_dim(padded, 2, keep + 2, axis=which_axis)
    )


def wind_rows(courants, cycle, component, offset, length):
    surface = courants[cycle, component]
    doubled = jnp.concatenate([surface, surface], axis=0)
    return lax.dynamic_slice_in_dim(doubled, jnp.mod(offset, surface.shape[0]), length, 0)


def lane_spread(x, k):
    return jnp.broadcast_to(x[:, k : k + 1], x.shape)


def row_spread(x, k):
    return jnp.broadcast_to(x[k : k + 1, :], x.shape)


def tree_sum(terms):
    while len(terms) > 1:
        terms = [a + b for a, b in zip(terms[::2], terms[1::2])]
    return terms[0]


def inverse_tile(rows, lane, sub):
    rows = list(rows)
    for g in range(TILE // GROUP):
        panel = rows[g]
        first = GROUP * g
        inside = (lane >= first) & (lane < first + GROUP)
        cols = [lane_spread(panel, first + m) for m in range(GROUP)]
        for k in range(GROUP):
            here = sub == k
            flip = pl.reciprocal(row_spread(cols[k], k), approx=False)
            lead = cols[k]
            for m in range(GROUP):
                if m != k:
                    scaled = row_spread(cols[m], k) * flip
                    cols[m] = jnp.where(here, scaled, cols[m] - lead * scaled)
            cols[k] = jnp.where(here, flip, -lead * flip)
        panel = jnp.where(inside, jnp.where(lane - first == sub, 1.0, 0.0), panel)
        solved = tree_sum([cols[m] * row_spread(panel, m) for m in range(GROUP)])
        spread = [row_spread(solved, m) for m in range(GROUP)]
        for i in list(range(g + 1, len(rows))) + list(range(g)):
            change = tree_sum([lane_spread(rows[i], first + m) * spread[m] for m in range(GROUP)])
            rows[i] = jnp.where(inside, 0.0, rows[i]) - change
        rows[g] = solved
    return rows


def exact_dot(a, b):
    return jnp.dot(a, b, precision=finest_accuracy, preferred_element_type=jnp.float32)


def solve_kernel(slabs_ref, noise_ref, out_ref, work):
    size = noise_ref.shape[1]
    lane = lax.broadcasted_iota(jnp.int32, (GROUP, TILE), 1)
    sub = lax.broadcasted_iota(jnp.int32, (GROUP, TILE), 0)
    slabs, share = slabs_ref.shape[0], slabs_ref.shape[1] // HALVES
    for n in range(slabs):
        for half in range(HALVES):
            place = (n // CORES * HALVES + half) * CORES + n % CORES
            work[place * share : (place + 1) * share, :] = slabs_ref[
                n, half * share : (half + 1) * share, :
            ]
    square = work[:, :size]
    square = 0.5 * (square + square.T)
    diagonal = lax.broadcasted_iota(jnp.int32, (size, size), 0) == lax.broadcasted_iota(
        jnp.int32, (size, size), 1
    )
    work[:, :size] = jnp.where(diagonal, square + noise_ref[...], square)
    tiles = size // TILE
    spans = [slice(t * TILE, (t + 1) * TILE) for t in range(tiles)]
    held = None
    for t in range(tiles + 1):
        if t < tiles:
            here, rest = spans[t], (t + 1) * TILE
            square = work[here, here]
            if held is not None:
                square = square - exact_dot(work[here, spans[t - 1]], held[:, :TILE])
            rows = [square[GROUP * i : GROUP * (i + 1)] for i in range(TILE // GROUP)]
            inverse = jnp.concatenate(inverse_tile(rows, lane, sub), axis=0)
        if held is not None:
            column = slice(t * TILE, work.shape[1])
            for i in range(tiles):
                if i != t - 1:
                    work[spans[i], column] = work[spans[i], column] - exact_dot(
                        work[spans[i], spans[t - 1]], held
                    )
            work[spans[t - 1], column] = held
        if t < tiles:
            held = exact_dot(inverse, work[here, rest:])
    out_ref[...] = work[:, size:]


def solve_gain(slabs, noise):
    size, wide = noise.shape[0], slabs.shape[2]
    return pl.pallas_call(
        solve_kernel,
        out_shape=jax.ShapeDtypeStruct((size, wide - size), jnp.float32),
        in_specs=[pl.BlockSpec(memory_space=pltpu.VMEM)] * 2,
        out_specs=pl.BlockSpec(memory_space=pltpu.VMEM),
        scratch_shapes=[pltpu.VMEM((size, wide), jnp.float32)],
        name="solve_gain",
    )(slabs, noise[None, :])


def columns_kernel(*refs):
    fields, winds, (noise_ref, shift_ref, out_ref) = refs[:4], refs[4:8], refs[8:]
    height = out_ref.shape[0]
    for start in range(0, height, STRIP):
        strip = slice(start, start + STRIP)
        tiles = [
            ref[strip, k * NC : (k + 1) * NC]
            for ref in fields
            for k in range(ref.shape[1] // NC)
        ]
        for cycle in range(CYCLES):
            east, north = winds[2 * cycle][...], winds[2 * cycle + 1][...]
            behind, centre, ahead = stencil_weights(east)
            tiles = [
                behind[i : i + 1] * pltpu.roll(tile, 1, 1)
                + centre[i : i + 1] * tile
                + ahead[i : i + 1] * pltpu.roll(tile, NC - 1, 1)
                for i, tile in enumerate(tiles)
            ]
            behind, centre, ahead = stencil_weights(north)
            tiles = [
                behind[i : i + 1] * tiles[i]
                + centre[i : i + 1] * tiles[i + 1]
                + ahead[i : i + 1] * tiles[i + 2]
                for i in range(len(tiles) - 2)
            ]
        row = lax.broadcasted_iota(jnp.int32, (STRIP, NC), 0) + (shift_ref[0] + start)
        column = lax.broadcasted_iota(jnp.int32, (STRIP, NC), 1)
        for i, tile in enumerate(tiles):
            here = slice(i * NC, (i + 1) * NC)
            out_ref[strip, here] = tile + jnp.where(
                row == column + i * NC, noise_ref[:, here], 0.0
            )


def columns_forecast(fields, winds, noise, shift):
    height = fields[0].shape[0]
    return pl.pallas_call(
        columns_kernel,
        out_shape=jax.ShapeDtypeStruct((height, noise.shape[1]), jnp.float32),
        in_specs=[pl.BlockSpec(memory_space=pltpu.VMEM)] * 9
        + [pl.BlockSpec(memory_space=pltpu.SMEM)],
        out_specs=pl.BlockSpec(memory_space=pltpu.VMEM),
        name="columns_forecast",
    )(*fields, *winds, noise, shift)


def contract(a, b, dims):
    return lax.dot_general(a, b, (dims, ((), ())), precision=finest_accuracy)


def step_rows(field, courants, cycle, first):
    length = field.shape[0]
    field = sweep_local(field, wind_rows(courants, cycle, 0, first, length)[:, :, None], 1)
    north = wind_rows(courants, cycle, 1, first + 1, length - 2)[:, :, None]
    return sweep_padded(field, north, 0)


def by_shifts(part, axis):
    size, mine = lax.axis_size(axis), lax.axis_index(axis)
    parts = jnp.zeros((size, *part.shape), part.dtype)
    parts = lax.dynamic_update_index_in_dim(parts, part, mine, 0)
    for shift in range(1, size):
        got = lax.ppermute(part, axis, [(i, (i + shift) % size) for i in range(size)])
        parts = lax.dynamic_update_index_in_dim(parts, got, jnp.mod(mine - shift, size), 0)
    return parts


def one_cycle(covariance, courants, process_noise_spread, sensor_targets, noise_variance):
    row_index, column_index = lax.axis_index(ROW), lax.axis_index(COL)
    height, width = covariance.shape
    band_rows, band_columns = height // NC, width // NC
    row_first, column_first = row_index * band_rows, column_index * band_columns
    edge = CYCLES * NC

    halves = []
    for part in (covariance[:, width - edge :], covariance[:, :edge]):
        before, after = from_neighbours(part[:edge], part[height - edge :], ROW)
        if halves:
            before, after, _ = lax.optimization_barrier((before, after, halves[0]))
        field = jnp.concatenate([before, part, after], axis=0).reshape(-1, NC, edge)
        for cycle in range(CYCLES):
            field = step_rows(field, courants, cycle, row_first - CYCLES + cycle)
        halves.append(field.reshape(height, edge))
    upper, lower = halves
    before, after = from_neighbours(lower, upper, COL)
    winds = []
    for cycle in range(CYCLES):
        first, length = column_first - CYCLES + cycle, band_columns + 2 * (CYCLES - cycle)
        winds.append(wind_rows(courants, cycle, 0, first, length))
        winds.append(wind_rows(courants, cycle, 1, first + 1, length - 2))
    noise_here = process_noise_spread.reshape(1, height)
    offset = row_first - column_first
    noise_columns = jnp.concatenate(
        [jnp.where(offset == k, noise_here, 0.0) for k in range(0, band_columns, band_rows)], axis=1
    )
    forecast = columns_forecast(
        (before, lower, upper, after), winds, noise_columns, jnp.reshape(offset * NC, (1,))
    )
    row_ids = row_index * height + jnp.arange(height, dtype=jnp.int32)
    column_ids = column_index * width + jnp.arange(width, dtype=jnp.int32)

    sensors = sensor_targets.shape[0]
    row_share = sensors // lax.axis_size(ROW)
    column_share = sensors // lax.axis_size(COL)
    row_sensors = lax.dynamic_slice_in_dim(sensor_targets, row_index * row_share, row_share)
    column_sensors = lax.dynamic_slice_in_dim(
        sensor_targets, column_index * column_share, column_share
    )
    pick_rows = (row_sensors[:, None] == row_ids[None, :]).astype(jnp.float32)
    pick_columns = (column_sensors[:, None] == column_ids[None, :]).astype(jnp.float32)
    obs = contract(pick_rows, forecast, ((1,), (0,)))
    block = contract(obs, pick_columns, ((1,), (1,)))
    gain = contract(pick_columns, forecast, ((1,), (1,)))

    high = lax.axis_size("zh")
    block = from_everyone(block.reshape(-1, NC), ("y", "zl", "zh"))
    gain = by_shifts(gain, "zh").reshape(-1, height)
    block, gain, obs = lax.optimization_barrier((block, gain, obs))
    block = block.reshape(-1, high, row_share, column_share)
    slab = block.transpose(1, 3, 0, 2).reshape(high * column_share, sensors)
    slabs = from_everyone(jnp.concatenate([slab, gain], axis=1), ("x", "core"))

    obs = by_shifts(obs, "zl").reshape(-1, width)
    slabs, obs = lax.optimization_barrier((slabs, obs))
    obs_rows = from_everyone(obs, "y").reshape(sensors, width)
    solved = solve_gain(slabs, noise_variance)
    return forecast - contract(solved, obs_rows, ((0,), (0,)))


ROW = ("y", "zl")
COL = ("x", "zh", "core")


def physical(mesh):
    rows, columns = mesh.devices.shape
    zl, zh, core = 4, HALVES, CORES
    shape = (rows // zl, zl, columns // (zh * core), zh, core)
    return jax.sharding.Mesh(mesh.devices.reshape(shape), ROW + COL)


def solution(mesh):
    in_specs = (P(ROW, COL), P(), P(ROW, None), P(), P())
    out_specs = P(ROW, COL)
    return jax.shard_map(
        one_cycle, mesh=physical(mesh), in_specs=in_specs, out_specs=out_specs, check_vma=False
    )
```

```python
import jax
import jax.numpy as jnp
from jax import lax
from jax.experimental import pallas as pl
from jax.experimental.pallas import tpu as pltpu
from jax.sharding import PartitionSpec as P

NC = 128
CYCLES = 2
TILE = 128
GROUP = 8
STRIP = 64
CORES = 2
HALVES = 2


finest_accuracy = lax.Precision.HIGHEST


def from_everyone(array, axis):
    copies = jnp.broadcast_to(array, (lax.axis_size(axis), *array.shape))
    return lax.all_to_all(copies, axis, split_axis=0, concat_axis=0, tiled=True)


def from_neighbours(lower, upper, axis):
    size = lax.axis_size(axis)
    up = [(i, (i + 1) % size) for i in range(size)]
    down = [(j, i) for i, j in up]
    return lax.ppermute(upper, axis, up), lax.ppermute(lower, axis, down)


def stencil_weights(courant):
    return (
        courant * (1.0 + courant) * 0.5,
        1.0 - courant * courant,
        courant * (courant - 1.0) * 0.5,
    )


def sweep_local(field, courant, which_axis):
    weight_behind, weight_centre, weight_ahead = stencil_weights(courant)
    return (
        weight_behind * jnp.roll(field, 1, which_axis)
        + weight_centre * field
        + weight_ahead * jnp.roll(field, -1, which_axis)
    )


def sweep_padded(padded, courant, which_axis):
    keep = padded.shape[which_axis] - 2
    weight_behind, weight_centre, weight_ahead = stencil_weights(courant)
    return (
        weight_behind * lax.slice_in_dim(padded, 0, keep, axis=which_axis)
        + weight_centre * lax.slice_in_dim(padded, 1, keep + 1, axis=which_axis)
        + weight_ahead * lax.slice_in_dim(padded, 2, keep + 2, axis=which_axis)
    )


def wind_rows(courants, cycle, component, offset, length):
    surface = courants[cycle, component]
    doubled = jnp.concatenate([surface, surface], axis=0)
    return lax.dynamic_slice_in_dim(doubled, jnp.mod(offset, surface.shape[0]), length, 0)


def lane_spread(x, k):
    return jnp.broadcast_to(x[:, k : k + 1], x.shape)


def row_spread(x, k):
    return jnp.broadcast_to(x[k : k + 1, :], x.shape)


def tree_sum(terms):
    while len(terms) > 1:
        terms = [a + b for a, b in zip(terms[::2], terms[1::2])]
    return terms[0]


def inverse_tile(rows, lane, sub):
    rows = list(rows)
    for g in range(TILE // GROUP):
        panel = rows[g]
        first = GROUP * g
        inside = (lane >= first) & (lane < first + GROUP)
        cols = [lane_spread(panel, first + m) for m in range(GROUP)]
        for k in range(GROUP):
            here = sub == k
            flip = pl.reciprocal(row_spread(cols[k], k), approx=False)
            lead = cols[k]
            for m in range(GROUP):
                if m != k:
                    scaled = row_spread(cols[m], k) * flip
                    cols[m] = jnp.where(here, scaled, cols[m] - lead * scaled)
            cols[k] = jnp.where(here, flip, -lead * flip)
        panel = jnp.where(inside, jnp.where(lane - first == sub, 1.0, 0.0), panel)
        solved = tree_sum([cols[m] * row_spread(panel, m) for m in range(GROUP)])
        spread = [row_spread(solved, m) for m in range(GROUP)]
        for i in list(range(g + 1, len(rows))) + list(range(g)):
            change = tree_sum([lane_spread(rows[i], first + m) * spread[m] for m in range(GROUP)])
            rows[i] = jnp.where(inside, 0.0, rows[i]) - change
        rows[g] = solved
    return rows


def exact_dot(a, b):
    return jnp.dot(a, b, precision=finest_accuracy, preferred_element_type=jnp.float32)


def solve_kernel(mine_ref, other_ref, noise_ref, core_ref, out_ref, work):
    size = noise_ref.shape[1]
    lane = lax.broadcasted_iota(jnp.int32, (GROUP, TILE), 1)
    sub = lax.broadcasted_iota(jnp.int32, (GROUP, TILE), 0)
    share = mine_ref.shape[1] // HALVES
    for ref, core in ((mine_ref, core_ref[0]), (other_ref, 1 - core_ref[0])):
        for n in range(ref.shape[0]):
            for half in range(HALVES):
                place = (n * HALVES + half) * CORES + core
                work[pl.ds(pl.multiple_of(place * share, share), share), :] = ref[
                    n, half * share : (half + 1) * share, :
                ]
    square = work[:, :size]
    square = 0.5 * (square + square.T)
    diagonal = lax.broadcasted_iota(jnp.int32, (size, size), 0) == lax.broadcasted_iota(
        jnp.int32, (size, size), 1
    )
    work[:, :size] = jnp.where(diagonal, square + noise_ref[...], square)
    tiles = size // TILE
    spans = [slice(t * TILE, (t + 1) * TILE) for t in range(tiles)]
    held = None
    for t in range(tiles + 1):
        if t < tiles:
            here, rest = spans[t], (t + 1) * TILE
            square = work[here, here]
            if held is not None:
                square = square - exact_dot(work[here, spans[t - 1]], held[:, :TILE])
            rows = [square[GROUP * i : GROUP * (i + 1)] for i in range(TILE // GROUP)]
            inverse = jnp.concatenate(inverse_tile(rows, lane, sub), axis=0)
        if held is not None:
            column = slice(t * TILE, work.shape[1])
            for i in range(tiles):
                if i != t - 1:
                    work[spans[i], column] = work[spans[i], column] - exact_dot(
                        work[spans[i], spans[t - 1]], held
                    )
            work[spans[t - 1], column] = held
        if t < tiles:
            held = exact_dot(inverse, work[here, rest:])
    out_ref[...] = work[:, size:]


def solve_gain(mine, other, noise, core):
    size, wide = noise.shape[0], mine.shape[2]
    return pl.pallas_call(
        solve_kernel,
        out_shape=jax.ShapeDtypeStruct((size, wide - size), jnp.float32),
        in_specs=[pl.BlockSpec(memory_space=pltpu.VMEM)] * 3
        + [pl.BlockSpec(memory_space=pltpu.SMEM)],
        out_specs=pl.BlockSpec(memory_space=pltpu.VMEM),
        scratch_shapes=[pltpu.VMEM((size, wide), jnp.float32)],
        name="solve_gain",
    )(mine, other, noise[None, :], jnp.reshape(core, (1,)))


def columns_kernel(*refs):
    fields, winds, (noise_ref, shift_ref, out_ref) = refs[:4], refs[4:8], refs[8:]
    height = out_ref.shape[0]
    for start in range(0, height, STRIP):
        strip = slice(start, start + STRIP)
        tiles = [
            ref[strip, k * NC : (k + 1) * NC]
            for ref in fields
            for k in range(ref.shape[1] // NC)
        ]
        for cycle in range(CYCLES):
            east, north = winds[2 * cycle][...], winds[2 * cycle + 1][...]
            behind, centre, ahead = stencil_weights(east)
            tiles = [
                behind[i : i + 1] * pltpu.roll(tile, 1, 1)
                + centre[i : i + 1] * tile
                + ahead[i : i + 1] * pltpu.roll(tile, NC - 1, 1)
                for i, tile in enumerate(tiles)
            ]
            behind, centre, ahead = stencil_weights(north)
            tiles = [
                behind[i : i + 1] * tiles[i]
                + centre[i : i + 1] * tiles[i + 1]
                + ahead[i : i + 1] * tiles[i + 2]
                for i in range(len(tiles) - 2)
            ]
        row = lax.broadcasted_iota(jnp.int32, (STRIP, NC), 0) + (shift_ref[0] + start)
        column = lax.broadcasted_iota(jnp.int32, (STRIP, NC), 1)
        for i, tile in enumerate(tiles):
            here = slice(i * NC, (i + 1) * NC)
            out_ref[strip, here] = tile + jnp.where(
                row == column + i * NC, noise_ref[:, here], 0.0
            )


def columns_forecast(fields, winds, noise, shift):
    height = fields[0].shape[0]
    return pl.pallas_call(
        columns_kernel,
        out_shape=jax.ShapeDtypeStruct((height, noise.shape[1]), jnp.float32),
        in_specs=[pl.BlockSpec(memory_space=pltpu.VMEM)] * 9
        + [pl.BlockSpec(memory_space=pltpu.SMEM)],
        out_specs=pl.BlockSpec(memory_space=pltpu.VMEM),
        name="columns_forecast",
    )(*fields, *winds, noise, shift)


def contract(a, b, dims):
    return lax.dot_general(a, b, (dims, ((), ())), precision=finest_accuracy)


def step_rows(field, courants, cycle, first):
    length = field.shape[0]
    field = sweep_local(field, wind_rows(courants, cycle, 0, first, length)[:, :, None], 1)
    north = wind_rows(courants, cycle, 1, first + 1, length - 2)[:, :, None]
    return sweep_padded(field, north, 0)


def by_shifts(part, axis):
    size, mine = lax.axis_size(axis), lax.axis_index(axis)
    parts = jnp.zeros((size, *part.shape), part.dtype)
    parts = lax.dynamic_update_index_in_dim(parts, part, mine, 0)
    for shift in range(1, size):
        got = lax.ppermute(part, axis, [(i, (i + shift) % size) for i in range(size)])
        parts = lax.dynamic_update_index_in_dim(parts, got, jnp.mod(mine - shift, size), 0)
    return parts


def one_cycle(covariance, courants, process_noise_spread, sensor_targets, noise_variance):
    row_index, column_index = lax.axis_index(ROW), lax.axis_index(COL)
    height, width = covariance.shape
    band_rows, band_columns = height // NC, width // NC
    row_first, column_first = row_index * band_rows, column_index * band_columns
    edge = CYCLES * NC

    halves = []
    for part in (covariance[:, width - edge :], covariance[:, :edge]):
        before, after = from_neighbours(part[:edge], part[height - edge :], ROW)
        if halves:
            before, after, _ = lax.optimization_barrier((before, after, halves[0]))
        field = jnp.concatenate([before, part, after], axis=0).reshape(-1, NC, edge)
        for cycle in range(CYCLES):
            field = step_rows(field, courants, cycle, row_first - CYCLES + cycle)
        halves.append(field.reshape(height, edge))
    upper, lower = halves
    before, after = from_neighbours(lower, upper, COL)
    winds = []
    for cycle in range(CYCLES):
        first, length = column_first - CYCLES + cycle, band_columns + 2 * (CYCLES - cycle)
        winds.append(wind_rows(courants, cycle, 0, first, length))
        winds.append(wind_rows(courants, cycle, 1, first + 1, length - 2))
    noise_here = process_noise_spread.reshape(1, height)
    offset = row_first - column_first
    noise_columns = jnp.concatenate(
        [jnp.where(offset == k, noise_here, 0.0) for k in range(0, band_columns, band_rows)], axis=1
    )
    forecast = columns_forecast(
        (before, lower, upper, after), winds, noise_columns, jnp.reshape(offset * NC, (1,))
    )
    row_ids = row_index * height + jnp.arange(height, dtype=jnp.int32)
    column_ids = column_index * width + jnp.arange(width, dtype=jnp.int32)

    sensors = sensor_targets.shape[0]
    row_share = sensors // lax.axis_size(ROW)
    column_share = sensors // lax.axis_size(COL)
    row_sensors = lax.dynamic_slice_in_dim(sensor_targets, row_index * row_share, row_share)
    column_sensors = lax.dynamic_slice_in_dim(
        sensor_targets, column_index * column_share, column_share
    )
    pick_rows = (row_sensors[:, None] == row_ids[None, :]).astype(jnp.float32)
    pick_columns = (column_sensors[:, None] == column_ids[None, :]).astype(jnp.float32)
    obs = contract(pick_rows, forecast, ((1,), (0,)))
    block = contract(obs, pick_columns, ((1,), (1,)))
    gain = contract(pick_columns, forecast, ((1,), (1,)))

    high = lax.axis_size("zh")
    block = from_everyone(block.reshape(-1, NC), ("y", "zl", "zh"))
    gain = by_shifts(gain, "zh").reshape(-1, height)
    block, gain, obs = lax.optimization_barrier((block, gain, obs))
    block = block.reshape(-1, high, row_share, column_share)
    slab = block.transpose(1, 3, 0, 2).reshape(high * column_share, sensors)
    mine = from_everyone(jnp.concatenate([slab, gain], axis=1), "x")

    mine, obs = lax.optimization_barrier((mine, obs))
    other = lax.ppermute(mine, "core", [(0, 1), (1, 0)])
    obs_rows = from_everyone(obs, ROW).reshape(sensors, width)
    solved = solve_gain(mine, other, noise_variance, lax.axis_index("core"))
    return forecast - contract(solved, obs_rows, ((0,), (0,)))


ROW = ("y", "zl")
COL = ("x", "zh", "core")


def physical(mesh):
    rows, columns = mesh.devices.shape
    zl, zh, core = 4, HALVES, CORES
    shape = (rows // zl, zl, columns // (zh * core), zh, core)
    return jax.sharding.Mesh(mesh.devices.reshape(shape), ROW + COL)


def solution(mesh):
    in_specs = (P(ROW, COL), P(), P(ROW, None), P(), P())
    out_specs = P(ROW, COL)
    return jax.shard_map(
        one_cycle, mesh=physical(mesh), in_specs=in_specs, out_specs=out_specs, check_vma=False
    )
```
